256 devices in a mesh: past: 32 (over y, x, core), second: 8 (over z).
Axes of the slice: x: 4, y: 4, z: 8, core: 2. Of those that a mesh axis runs over, the one named last changes fastest.
Arguments:
- g_hist: bfloat16 [65536, 8192], P('past', 'second'), may hold values from -6 to 6
- sigma_hist: bfloat16 [1024, 65536], P(None, 'past'), may hold values from -0.046875 to 0.046875
- volterra: bfloat16 [2, 512, 1024], replicated, may hold values from -0.1875 to 0.1875
- sigma_edge: bfloat16 [512, 8192], P(None, 'second'), may hold values from -6 to 6
- coupling: float32 [32, 8192], P(None, 'second'), may hold values from 0.3 to 3
Outputs:
- g_new: bfloat16 [1024, 8192], P(None, 'second')
- sigma_new: bfloat16 [1024, 8192], P(None, 'second')
The draws below stay inside these ranges and needn't reach their ends.
All inputs are finite; a program needn't handle non-finite values.
Results may differ from the reference program's by a relative error of at most 0.0059.
Values may be sent and summed in bfloat16 or wider, within the bound.
A program may use at most 64 MiB of HBM per device.

```python
import math
import jax
import jax.numpy as jnp

N = 32
BLK = 16
NB = 2
NS = 2048
NC = 256


def with_spikes(values, own_key, source, target, parts, factor):
    owner, partner = [(jnp.arange(values.shape[dim]) // (values.shape[dim] // parts)).reshape([-1 if axis == dim else 1 for axis in range(values.ndim)]) for dim in (source, target)]
    chosen = jax.random.permutation(own_key, parts)[partner]
    strong = (owner == chosen) | (owner == (partner + parts // 2) % parts)
    return jnp.where(strong, factor * values, values)


def shard_levels(stream_key, extent, split, low, largest):
    def one(dim, blocks):
        draws = jax.random.uniform(jax.random.fold_in(jax.random.fold_in(stream_key, 6), dim), (blocks,), jnp.float32, low / len(split), largest / len(split))
        return jnp.repeat(jnp.exp(draws), extent[dim] // blocks).reshape((-1,) + (1,) * (len(extent) - dim - 1))

    gain = one(*split[0])
    for cut in split[1:]:
        gain = gain * one(*cut)
    return gain


def gaussian(stream_key, shape, deviation, bound, pieces=(), dtype=jnp.bfloat16):
    drawn = jax.random.normal(stream_key, shape, jnp.float32) * deviation
    if len(pieces) > 0:
        drawn = shard_levels(stream_key, shape, pieces, -0.22, 0.18) * drawn
    return jnp.clip(drawn, min=-bound, max=bound).astype(dtype)


def noise_with(rng, dims, scale, bound, cuts, heavy, kind=jnp.bfloat16):
    entries = scale * jax.random.normal(rng, dims, jnp.float32)
    if cuts:
        entries = entries * shard_levels(rng, dims, cuts, -0.22, 0.18)
    return jnp.clip(with_spikes(entries, jax.random.fold_in(rng, 3), *heavy), -bound, bound).astype(kind)


def setup_inputs(seed: int = 0) -> dict:
    streams_of = jax.random.split(jax.random.key(seed), 6)
    return {
        "g_hist": gaussian(streams_of[0], (NS * N, NC * N), 1.0, 6.0, ((0, 32), (1, 8))),
        "sigma_hist": noise_with(streams_of[1], (NB * BLK * N, NS * N), (NS * N) ** -0.5, 0.046875, ((1, 32),), (1, 0, 32, 2.75)),
        "volterra": gaussian(streams_of[2], (NB, BLK * N, 2 * BLK * N), (2 * BLK * N) ** -0.5, 0.1875),
        "sigma_edge": gaussian(streams_of[3], (BLK * N, NC * N), 1.0, 6.0, ((1, 8),)),
        "coupling": jnp.clip(jnp.exp(math.log(3.0) - 2.3025851 * jax.random.uniform(streams_of[4], (N, NC * N), jnp.float32) ** shard_levels(streams_of[4], (N, NC * N), ((1, 8),), -0.2, 0.2)), 0.3, 3.0),
    }


def reference(g_hist, sigma_hist, volterra, sigma_edge, coupling):
    rows = BLK * N
    prev = sigma_edge
    g_blocks = []
    s_blocks = []
    for block in range(NB):
        sig_rows = sigma_hist[block * rows:(block + 1) * rows, :]
        memory = jnp.dot(sig_rows, g_hist, preferred_element_type=jnp.float32).astype(jnp.bfloat16)
        stacked = jnp.concatenate([memory, prev], axis=0)
        gnew = jnp.dot(volterra[block], stacked, preferred_element_type=jnp.float32)
        cubic = gnew.reshape(BLK, N, -1) ** 3 * coupling[None]
        meansq = jnp.mean(cubic * cubic)
        sigma = (cubic / jnp.sqrt(meansq + 1e-06)).reshape(rows, -1).astype(jnp.bfloat16)
        g_blocks.append(gnew.astype(jnp.bfloat16))
        s_blocks.append(sigma)
        prev = sigma
    return (jnp.concatenate(g_blocks, axis=0), jnp.concatenate(s_blocks, axis=0))
```

```python
import functools

import jax
import jax.numpy as jnp
from jax import lax
from jax.experimental import pallas as pl
from jax.experimental.pallas import tpu as pltpu
from jax.sharding import PartitionSpec as P

N = 32
MESH = pl.DeviceIdType.MESH
F32 = jnp.float32
BF16 = jnp.bfloat16
RING = 4
CHUNKS = 4


def dot(a, b):
    return jnp.dot(a, b, preferred_element_type=F32)


def kernel(
    n_z, count_all,
    g_hbm, sig_hbm, vol_hbm, edge_hbm, coup_hbm, g_out, s_out,
    g, sig, vol, edge, coup, psend, precv, own, a_buf, ra, a2, rb, b_buf, b_f32, rc, mem, s_buf, cubic, stat,
    send_sem, recv_sem, load_sem,
):
    rows = mem.shape[1]
    half = rows // 2
    sub = half // RING
    hs = sub // 2
    piece = sub // RING
    width = mem.shape[2]
    tile = min(256, width)

    past = lax.axis_index("past")
    z = lax.axis_index("second")
    core = lax.rem(past, 2)
    x = lax.rem(past // 2, RING)
    y = past // (2 * RING)
    s = x * (1 - core) + y * core
    t = y * (1 - core) + x * core

    def device(s_, t_):
        return ((t_ * RING + s_) * 2 * (1 - core) + ((s_ * RING + t_) * 2 + 1) * core, z)

    right_s, left_s, opp_s = lax.rem(s + 1, RING), lax.rem(s + 3, RING), lax.rem(s + 2, RING)
    right, left = device(right_s, t), device(left_s, t)
    partner = (past + 1 - 2 * core, z)
    t_of = [lax.rem(t + d, RING) for d in range(RING)]
    t_peer = [device(s, t_of[d]) for d in range(RING)]
    z_of = [lax.rem(z + d, n_z) for d in range(n_z)]
    z_peer = [(past, z_of[d]) for d in range(n_z)]

    loads = []

    def load(src, dst):
        copy = pltpu.make_async_copy(src, dst, load_sem.at[len(loads)])
        copy.start()
        loads.append(copy)
        return copy

    def sig_rows(b, part):
        return pl.ds(pl.multiple_of(b * rows + part * half, half), half)

    ld = {}
    ld["p0"] = load(sig_hbm.at[sig_rows(0, 1 - core)], sig.at[sig_rows(0, 1 - core)])
    ld["g0"] = load(g_hbm.at[:, 0:width], g.at[0])
    ld["o0"] = load(sig_hbm.at[sig_rows(0, core)], sig.at[sig_rows(0, core)])
    ld["g1"] = load(g_hbm.at[:, width : 2 * width], g.at[1])

    def load_rest():
        ld["p1"] = load(sig_hbm.at[sig_rows(1, 1 - core)], sig.at[sig_rows(1, 1 - core)])
        ld["o1"] = load(sig_hbm.at[sig_rows(1, core)], sig.at[sig_rows(1, core)])
        ld["edge"] = load(edge_hbm, edge)
        ld["vol"] = load(vol_hbm, vol)
        ld["coup"] = load(coup_hbm, coup)

    barrier = pltpu.get_barrier_semaphore()
    friends = [partner, right, left] + t_peer[1:] + z_peer[1:]
    for friend in friends:
        pl.semaphore_signal(barrier, inc=1, device_id=friend, device_id_type=MESH)

    sends = []
    ids = {}

    def sem_id(name):
        return ids.setdefault(name, len(ids))

    def put(name, src, dst, to):
        i = sem_id(name)
        copy = pltpu.make_async_remote_copy(
            src_ref=src, dst_ref=dst, send_sem=send_sem.at[i], recv_sem=recv_sem.at[i],
            device_id=to, device_id_type=MESH,
        )
        copy.start()
        sends.append(copy)

    def arrived(name, dst):
        i = sem_id(name)
        pltpu.make_async_remote_copy(
            src_ref=dst, dst_ref=dst, send_sem=send_sem.at[i], recv_sem=recv_sem.at[i],
            device_id=partner, device_id_type=MESH,
        ).wait_recv()

    def at(start, size):
        return pl.ds(pl.multiple_of(start, size), size)

    def product(k):
        b, j = k // 2, k % 2
        if j == 0:
            ld[f"p{b}"].wait()
        if b == 0:
            ld[f"g{j}"].wait()
        for i in range(width // tile):
            cols = pl.ds(i * tile, tile)
            psend[k, :, cols] = dot(sig[sig_rows(b, 1 - core)], g[j, :, cols]).astype(BF16)
        if k == 0:
            load_rest()
            pl.semaphore_wait(barrier, len(friends))
        put(("chip", k), psend.at[k], precv.at[k], partner)
        if j == 0:
            ld[f"o{b}"].wait()
        for i in range(width // tile):
            cols = pl.ds(i * tile, tile)
            own[k, :, cols] = dot(sig[sig_rows(b, core)], g[j, :, cols])

    def chip_sum(k):
        arrived(("chip", k), precv.at[k])
        a_buf[k] = (own[k] + precv[k].astype(F32)).astype(BF16)
        put(("a0", k), a_buf.at[k, at(opp_s * sub, hs)], ra.at[k, 0], right)
        put(("a1", k), a_buf.at[k, at(opp_s * sub + hs, hs)], ra.at[k, 1], left)
        put(("u0", k), a_buf.at[k, at(right_s * sub + hs, hs)], rb.at[k, 0, hs:sub], right)
        put(("u1", k), a_buf.at[k, at(left_s * sub, hs)], rb.at[k, 1, 0:hs], left)

    def ring_add(k):
        arrived(("a0", k), ra.at[k, 0])
        a2[k, 0] = (a_buf[k, at(right_s * sub, hs)].astype(F32) + ra[k, 0].astype(F32)).astype(BF16)
        put(("b0", k), a2.at[k, 0], rb.at[k, 0, 0:hs], right)
        arrived(("a1", k), ra.at[k, 1])
        a2[k, 1] = (a_buf[k, at(left_s * sub + hs, hs)].astype(F32) + ra[k, 1].astype(F32)).astype(BF16)
        put(("b1", k), a2.at[k, 1], rb.at[k, 1, hs:sub], left)

    def ring_sum(k):
        arrived(("u0", k), rb.at[k, 0, hs:sub])
        arrived(("u1", k), rb.at[k, 1, 0:hs])
        arrived(("b0", k), rb.at[k, 0, 0:hs])
        arrived(("b1", k), rb.at[k, 1, hs:sub])
        mine = at(s * sub, sub)
        total = (own[k, mine] + precv[k, mine].astype(F32)) + (rb[k, 0].astype(F32) + rb[k, 1].astype(F32))
        b_f32[k] = total
        b_buf[k] = total.astype(BF16)
        for d in range(1, RING):
            put(("c", k, d), b_buf.at[k, at(t_of[d] * piece, piece)], rc.at[k, d - 1], t_peer[d])

    def mem_at(k, part, s_, start, size):
        return mem.at[k, at(part * half + s_ * sub + start, size)]

    def piece_sum(k):
        total = b_f32[k, at(t * piece, piece)]
        for d in range(1, RING):
            arrived(("c", k, d), rc.at[k, d - 1])
            total = total + rc[k, d - 1].astype(F32)
        mem[k, at(core * half + s * sub + t * piece, piece)] = total.astype(BF16)
        for d in range(1, RING):
            ref = mem_at(k, core, s, t * piece, piece)
            put(("d", k, d), ref, ref, t_peer[d])

    def gather_first(k):
        for d in range(1, RING):
            arrived(("d", k, d), mem_at(k, core, s, t_of[RING - d] * piece, piece))
        ref = mem_at(k, core, s, 0, sub)
        put(("e0", k), ref, ref, right)
        put(("e1", k), ref, ref, left)
        put(("f0", k), ref, ref, partner)

    def gather_next(k):
        ref = mem_at(k, core, left_s, 0, sub)
        arrived(("e0", k), ref)
        low = mem_at(k, core, left_s, 0, hs)
        put(("h0", k), low, low, right)
        put(("f1", k), ref, ref, partner)
        ref = mem_at(k, core, right_s, 0, sub)
        arrived(("e1", k), ref)
        high = mem_at(k, core, right_s, hs, hs)
        put(("h1", k), high, high, left)
        put(("f2", k), ref, ref, partner)

    def gather_last(k):
        arrived(("h0", k), mem_at(k, core, opp_s, 0, hs))
        arrived(("h1", k), mem_at(k, core, opp_s, hs, hs))
        ref = mem_at(k, core, opp_s, 0, sub)
        put(("f3", k), ref, ref, partner)

    def gathered(k):
        arrived(("f0", k), mem_at(k, 1 - core, t, 0, sub))
        arrived(("f1", k), mem_at(k, 1 - core, t_of[3], 0, sub))
        arrived(("f2", k), mem_at(k, 1 - core, t_of[1], 0, sub))
        arrived(("f3", k), mem_at(k, 1 - core, t_of[2], 0, sub))

    def columns_of(k, i):
        return pl.ds((k % 2) * width + i * tile, tile)

    def fold(value):
        square = value * value
        part = jnp.sum(square.reshape(rows // 8, 8, tile), axis=0)
        out = part[:, 0:128]
        for i in range(1, tile // 128):
            out = out + part[:, i * 128 : (i + 1) * 128]
        return out

    def finish(b, cols, gnew):
        g_out[pl.ds(b * rows, rows), cols] = gnew.astype(BF16)
        cube = (gnew * gnew * gnew).reshape(rows // N, N, tile) * coup[:, cols][None]
        cube = cube.reshape(rows, tile)
        cubic[:, cols] = cube
        return fold(cube)

    def share(b, total):
        stat[b, z] = total
        for d in range(1, n_z):
            put(("z", b, d), stat.at[b, z], stat.at[b, z], z_peer[d])

    def scale_of(b):
        for d in range(1, n_z):
            arrived(("z", b, d), stat.at[b, z_of[n_z - d]])
        total = jnp.sum(jnp.sum(stat[b], axis=0))
        mean = total / count_all
        return jnp.sqrt(jnp.full((8, 128), mean + 1e-6, F32))[0:1, 0:1]

    def scaled(b, scale):
        inv = 1.0 / scale
        for i in range(2 * width // tile):
            cols = pl.ds(i * tile, tile)
            s_out[pl.ds(b * rows, rows), cols] = (cubic[:, cols] * inv).astype(BF16)

    def start_value():
        ld["edge"].wait()
        ld["vol"].wait()
        ld["coup"].wait()
        for i in range(2 * width // tile):
            cols = pl.ds(i * tile, tile)
            s_buf[0, :, cols] = dot(vol[0, :, rows : 2 * rows], edge[:, cols])

    def first_block(k):
        gathered(k)
        total = None
        for i in range(width // tile):
            cols = columns_of(k, i)
            gnew = s_buf[0, :, cols] + dot(vol[0, :, 0:rows], mem[k, :, pl.ds(i * tile, tile)])
            part = finish(0, cols, gnew)
            total = part if total is None else total + part
        return total

    def second_memory(k):
        gathered(k)
        for i in range(width // tile):
            s_buf[1, :, columns_of(k, i)] = dot(vol[1, :, 0:rows], mem[k, :, pl.ds(i * tile, tile)])

    stages = [chip_sum, ring_add, ring_sum, piece_sum, gather_first, gather_next, gather_last]
    sums = []
    for step in range(CHUNKS + len(stages) + 1):
        if step < CHUNKS:
            product(step)
        if step == CHUNKS:
            start_value()
        for k in range(CHUNKS):
            i = step - k - 1
            if 0 <= i < len(stages):
                stages[i](k)
            if i == len(stages):
                if k < 2:
                    sums.append(first_block(k))
                    if k == 1:
                        share(0, sums[0] + sums[1])
                else:
                    second_memory(k)

    scaled(0, scale_of(0))
    total = None
    for i in range(2 * width // tile):
        cols = pl.ds(i * tile, tile)
        gnew = s_buf[1, :, cols] + dot(vol[1, :, rows : 2 * rows], s_out[0:rows, cols])
        part = finish(1, cols, gnew)
        total = part if total is None else total + part
    share(1, total)
    scaled(1, scale_of(1))
    for copy in sends:
        copy.wait_send()


def per_device(g_hist, sigma_hist, volterra, sigma_edge, coupling):
    rows = volterra.shape[1]
    columns = g_hist.shape[1]
    depth = g_hist.shape[0]
    n_z = lax.axis_size("second")
    width = columns // 2
    half = rows // 2
    sub = half // RING
    piece = sub // RING
    n_sem = 21 * CHUNKS + 2 * (n_z - 1)
    vmem = pltpu.VMEM
    return pl.pallas_call(
        functools.partial(kernel, n_z, rows * columns * n_z),
        out_shape=[jax.ShapeDtypeStruct((2 * rows, columns), BF16)] * 2,
        in_specs=[pl.BlockSpec(memory_space=pl.ANY)] * 5,
        out_specs=[pl.BlockSpec(memory_space=pltpu.VMEM)] * 2,
        scratch_shapes=[
            vmem((2, depth, width), BF16),
            vmem((2 * rows, depth), BF16),
            vmem(volterra.shape, BF16),
            vmem(sigma_edge.shape, BF16),
            vmem(coupling.shape, F32),
            vmem((CHUNKS, half, width), BF16),
            vmem((CHUNKS, half, width), BF16),
            vmem((CHUNKS, half, width), F32),
            vmem((CHUNKS, half, width), BF16),
            vmem((CHUNKS, 2, sub // 2, width), BF16),
            vmem((CHUNKS, 2, sub // 2, width), BF16),
            vmem((CHUNKS, 2, sub, width), BF16),
            vmem((CHUNKS, sub, width), BF16),
            vmem((CHUNKS, sub, width), F32),
            vmem((CHUNKS, RING - 1, piece, width), BF16),
            vmem((CHUNKS, rows, width), BF16),
            vmem((2, rows, columns), F32),
            vmem((rows, columns), F32),
            vmem((2, n_z, 8, 128), F32),
            pltpu.SemaphoreType.DMA((n_sem,)),
            pltpu.SemaphoreType.DMA((n_sem,)),
            pltpu.SemaphoreType.DMA((9,)),
        ],
        compiler_params=pltpu.CompilerParams(
            collective_id=0, has_side_effects=True, vmem_limit_bytes=60 * 1024 * 1024
        ),
    )(g_hist, sigma_hist, volterra, sigma_edge, coupling)


def solution(mesh):
    return jax.shard_map(
        per_device,
        mesh=mesh,
        in_specs=(P("past", "second"), P(None, "past"), P(), P(None, "second"), P(None, "second")),
        out_specs=(P(None, "second"), P(None, "second")),
        check_vma=False,
    )
```

```python
import functools

import jax
import jax.numpy as jnp
from jax import lax
from jax.experimental import pallas as pl
from jax.experimental.pallas import tpu as pltpu
from jax.sharding import PartitionSpec as P

N = 32
MESH = pl.DeviceIdType.MESH
F32 = jnp.float32
BF16 = jnp.bfloat16
RING = 4
CHUNKS = 4


def dot(a, b):
    return jnp.dot(a, b, preferred_element_type=F32)


def kernel(
    n_z, count_all,
    g_hbm, sig_hbm, vol_hbm, edge_hbm, coup_hbm, g_out, s_out,
    g, sig, vol, edge, coup, psend, precv, own, a_buf, ra, b_buf, mem, s_buf, cubic, stat,
    send_sem, recv_sem, load_sem,
):
    rows = mem.shape[1]
    half = rows // 2
    sub = half // RING
    width = mem.shape[2]
    tile = min(256, width)

    past = lax.axis_index("past")
    z = lax.axis_index("second")
    core = lax.rem(past, 2)
    x = lax.rem(past // 2, RING)
    y = past // (2 * RING)
    partner = (past + 1 - 2 * core, z)
    x_of = [lax.rem(x + d, RING) for d in range(RING)]
    y_of = [lax.rem(y + d, RING) for d in range(RING)]
    x_peer = [((y * RING + x_of[d]) * 2 + core, z) for d in range(RING)]
    y_peer = [((y_of[d] * RING + x) * 2 + core, z) for d in range(RING)]
    s_of, t_of = [x_of, y_of], [y_of, x_of]
    s_peer, t_peer = [x_peer, y_peer], [y_peer, x_peer]
    z_of = [lax.rem(z + d, n_z) for d in range(n_z)]
    z_peer = [(past, z_of[d]) for d in range(n_z)]

    loads = []

    def load(src, dst):
        copy = pltpu.make_async_copy(src, dst, load_sem.at[len(loads)])
        copy.start()
        loads.append(copy)
        return copy

    def sig_rows(b, part):
        return pl.ds(pl.multiple_of(b * rows + part * half, half), half)

    ld = {}
    ld["p0"] = load(sig_hbm.at[sig_rows(0, 1 - core)], sig.at[sig_rows(0, 1 - core)])
    ld["g0"] = load(g_hbm.at[:, 0:width], g.at[0])
    ld["o0"] = load(sig_hbm.at[sig_rows(0, core)], sig.at[sig_rows(0, core)])
    ld["g1"] = load(g_hbm.at[:, width : 2 * width], g.at[1])

    def load_rest():
        ld["p1"] = load(sig_hbm.at[sig_rows(1, 1 - core)], sig.at[sig_rows(1, 1 - core)])
        ld["o1"] = load(sig_hbm.at[sig_rows(1, core)], sig.at[sig_rows(1, core)])
        ld["edge"] = load(edge_hbm, edge)
        ld["vol"] = load(vol_hbm, vol)
        ld["coup"] = load(coup_hbm, coup)

    barrier = pltpu.get_barrier_semaphore()
    friends = [partner] + x_peer[1:] + y_peer[1:] + z_peer[1:]
    for friend in friends:
        pl.semaphore_signal(barrier, inc=1, device_id=friend, device_id_type=MESH)

    sends = []
    ids = {}

    def sem_id(name):
        return ids.setdefault(name, len(ids))

    def put(name, src, dst, to):
        i = sem_id(name)
        copy = pltpu.make_async_remote_copy(
            src_ref=src, dst_ref=dst, send_sem=send_sem.at[i], recv_sem=recv_sem.at[i],
            device_id=to, device_id_type=MESH,
        )
        copy.start()
        sends.append(copy)

    def arrived(name, dst):
        i = sem_id(name)
        pltpu.make_async_remote_copy(
            src_ref=dst, dst_ref=dst, send_sem=send_sem.at[i], recv_sem=recv_sem.at[i],
            device_id=partner, device_id_type=MESH,
        ).wait_recv()

    def at(start, size):
        return pl.ds(pl.multiple_of(start, size), size)

    def product_send(k):
        b, j = k // 2, k % 2
        if j == 0:
            ld[f"p{b}"].wait()
        if b == 0:
            ld[f"g{j}"].wait()
        for i in range(width // tile):
            cols = pl.ds(i * tile, tile)
            psend[k, :, cols] = dot(sig[sig_rows(b, 1 - core)], g[j, :, cols])
        if k == 0:
            load_rest()
            pl.semaphore_wait(barrier, len(friends))
        put(("chip", k), psend.at[k], precv.at[k], partner)

    def product_own(k):
        b, j = k // 2, k % 2
        if j == 0:
            ld[f"o{b}"].wait()
        for i in range(width // tile):
            cols = pl.ds(i * tile, tile)
            own[k, :, cols] = dot(sig[sig_rows(b, core)], g[j, :, cols])

    def mine(k):
        return at(s_of[k % 2][0] * sub, sub)

    def chip_sum(k):
        arrived(("chip", k), precv.at[k])
        a_buf[k] = (own[k] + precv[k]).astype(BF16)
        for d in (2, 1, 3):
            put(("a", k, d), a_buf.at[k, at(s_of[k % 2][d] * sub, sub)], ra.at[k, d - 1], s_peer[k % 2][d])

    def ring_sum(k):
        t = t_of[k % 2]
        total = own[k, mine(k)] + precv[k, mine(k)]
        for d in (1, 3, 2):
            arrived(("a", k, d), ra.at[k, d - 1])
            total = total + ra[k, d - 1].astype(F32)
        b_buf[k, t[0]] = total.astype(BF16)
        for d in (2, 1, 3):
            put(("b", k, d), b_buf.at[k, t[0]], b_buf.at[k, t[0]], t_peer[k % 2][d])

    def mem_at(k, part, d):
        return mem.at[k, at(part * half + s_of[k % 2][d] * sub, sub)]

    def plane_sum(k):
        t = t_of[k % 2]
        for d in (1, 3, 2):
            arrived(("b", k, d), b_buf.at[k, t[RING - d]])
        total = b_buf[k, 0].astype(F32)
        for i in range(1, RING):
            total = total + b_buf[k, i].astype(F32)
        mem[k, at(core * half + s_of[k % 2][0] * sub, sub)] = total.astype(BF16)
        ref = mem_at(k, core, 0)
        for d in (2, 1, 3):
            put(("c", k, d), ref, ref, s_peer[k % 2][d])
        put(("f", k, 0), ref, ref, partner)

    def gather(k):
        for d in (1, 3, 2):
            ref = mem_at(k, core, RING - d)
            arrived(("c", k, d), ref)
            put(("f", k, RING - d), ref, ref, partner)

    def gathered(k):
        for d in (0, 3, 1, 2):
            arrived(("f", k, d), mem_at(k, 1 - core, d))

    def columns_of(k, i):
        return pl.ds((k % 2) * width + i * tile, tile)

    def fold(value):
        square = value * value
        part = jnp.sum(square.reshape(rows // 8, 8, tile), axis=0)
        out = part[:, 0:128]
        for i in range(1, tile // 128):
            out = out + part[:, i * 128 : (i + 1) * 128]
        return out

    def finish(b, cols, gnew):
        g_out[pl.ds(b * rows, rows), cols] = gnew.astype(BF16)
        cube = (gnew * gnew * gnew).reshape(rows // N, N, tile) * coup[:, cols][None]
        cube = cube.reshape(rows, tile)
        cubic[:, cols] = cube
        return fold(cube)

    def share(b, total):
        stat[b, z] = total
        for d in range(1, n_z):
            put(("z", b, d), stat.at[b, z], stat.at[b, z], z_peer[d])

    def scale_of(b):
        for d in range(1, n_z):
            arrived(("z", b, d), stat.at[b, z_of[n_z - d]])
        total = jnp.sum(jnp.sum(stat[b], axis=0))
        mean = total / count_all
        return jnp.sqrt(jnp.full((8, 128), mean + 1e-6, F32))[0:1, 0:1]

    def scaled(b, scale):
        inv = 1.0 / scale
        for i in range(2 * width // tile):
            cols = pl.ds(i * tile, tile)
            s_out[pl.ds(b * rows, rows), cols] = (cubic[:, cols] * inv).astype(BF16)

    def start_value():
        ld["edge"].wait()
        ld["vol"].wait()
        ld["coup"].wait()
        for i in range(2 * width // tile):
            cols = pl.ds(i * tile, tile)
            s_buf[0, :, cols] = dot(vol[0, :, rows : 2 * rows], edge[:, cols])

    def first_block(k):
        gathered(k)
        total = None
        for i in range(width // tile):
            cols = columns_of(k, i)
            gnew = s_buf[0, :, cols] + dot(vol[0, :, 0:rows], mem[k, :, pl.ds(i * tile, tile)])
            part = finish(0, cols, gnew)
            total = part if total is None else total + part
        return total

    def second_memory(k):
        gathered(k)
        for i in range(width // tile):
            s_buf[1, :, columns_of(k, i)] = dot(vol[1, :, 0:rows], mem[k, :, pl.ds(i * tile, tile)])

    product_send(0)
    product_own(0)
    for k in range(1, CHUNKS):
        product_send(k)
        chip_sum(k - 1)
        product_own(k)
    chip_sum(CHUNKS - 1)
    start_value()
    ring_sum(0)
    ring_sum(1)
    ring_sum(2)
    plane_sum(0)
    ring_sum(3)
    plane_sum(1)
    plane_sum(2)
    gather(0)
    plane_sum(3)
    gather(1)
    total = first_block(0)
    gather(2)
    total = total + first_block(1)
    share(0, total)
    gather(3)
    second_memory(2)
    second_memory(3)

    scaled(0, scale_of(0))
    total = None
    for i in range(2 * width // tile):
        cols = pl.ds(i * tile, tile)
        gnew = s_buf[1, :, cols] + dot(vol[1, :, rows : 2 * rows], s_out[0:rows, cols])
        part = finish(1, cols, gnew)
        total = part if total is None else total + part
    share(1, total)
    scaled(1, scale_of(1))
    for copy in sends:
        copy.wait_send()


def per_device(g_hist, sigma_hist, volterra, sigma_edge, coupling):
    rows = volterra.shape[1]
    columns = g_hist.shape[1]
    depth = g_hist.shape[0]
    n_z = lax.axis_size("second")
    width = columns // 2
    half = rows // 2
    sub = half // RING
    n_sem = 14 * CHUNKS + 2 * (n_z - 1)
    vmem = pltpu.VMEM
    return pl.pallas_call(
        functools.partial(kernel, n_z, rows * columns * n_z),
        out_shape=[pltpu.VMEM((2 * rows, columns), BF16)] * 2,
        in_specs=[pl.BlockSpec(memory_space=pltpu.HBM)] * 5,
        out_specs=[pl.BlockSpec(memory_space=pltpu.VMEM)] * 2,
        scratch_shapes=[
            vmem((2, depth, width), BF16),
            vmem((2 * rows, depth), BF16),
            vmem(volterra.shape, BF16),
            vmem(sigma_edge.shape, BF16),
            vmem(coupling.shape, F32),
            vmem((CHUNKS, half, width), F32),
            vmem((CHUNKS, half, width), F32),
            vmem((CHUNKS, half, width), F32),
            vmem((CHUNKS, half, width), BF16),
            vmem((CHUNKS, RING - 1, sub, width), BF16),
            vmem((CHUNKS, RING, sub, width), BF16),
            vmem((CHUNKS, rows, width), BF16),
            vmem((2, rows, columns), F32),
            vmem((rows, columns), F32),
            vmem((2, n_z, 8, 128), F32),
            pltpu.SemaphoreType.DMA((n_sem,)),
            pltpu.SemaphoreType.DMA((n_sem,)),
            pltpu.SemaphoreType.DMA((9,)),
        ],
        compiler_params=pltpu.CompilerParams(
            collective_id=0, has_side_effects=True, vmem_limit_bytes=62_800_000
        ),
    )(g_hist, sigma_hist, volterra, sigma_edge, coupling)


def solution(mesh):
    return jax.shard_map(
        per_device,
        mesh=mesh,
        in_specs=(P("past", "second"), P(None, "past"), P(), P(None, "second"), P(None, "second")),
        out_specs=(P(None, "second"), P(None, "second")),
        check_vma=False,
    )
```

```python
import functools

import jax
import jax.numpy as jnp
from jax import lax
from jax.experimental import pallas as pl
from jax.experimental.pallas import tpu as pltpu
from jax.sharding import PartitionSpec as P

N = 32
MESH = pl.DeviceIdType.MESH
F32 = jnp.float32
BF16 = jnp.bfloat16
RING = 4
CHUNKS = 4


def dot(a, b):
    return jnp.dot(a, b, preferred_element_type=F32)


def kernel(
    n_z, count_all,
    g_hbm, sig_hbm, vol_hbm, edge_hbm, coup_hbm, g_out, s_out,
    g, sig, vol, edge, coup, psend, precv, own, a_buf, ra, b_buf, mem, s_buf, cubic0, cubic, cube16, stat,
    send_sem, recv_sem, load_sem,
):
    rows = mem.shape[1]
    half = rows // 2
    sub = half // 2 // RING
    width = mem.shape[2]
    tile = min(256, width)

    past = lax.axis_index("past")
    z = lax.axis_index("second")
    core = lax.rem(past, 2)
    x = lax.rem(past // 2, RING)
    y = past // (2 * RING)
    partner = (past + 1 - 2 * core, z)
    def bits(p):
        return lax.rem((p + 1) // 2, 2), p // 2

    xi, xj = bits(x)
    yi, yj = bits(y)

    def flip(bit, yes):
        return 1 - bit if yes else bit

    def position(i, j):
        return i + j * (3 - 2 * i)

    def face_of(f, d):
        dx, dy = d % 2, d // 2
        if f == 0:
            bx, by = flip(xi, dx), flip(yi, dy)
            px, py = position(bx, xj), position(by, yj)
        else:
            bx, by = flip(xj, dx), flip(yj, dy)
            px, py = position(xi, bx), position(yi, by)
        return bx + 2 * by, ((py * RING + px) * 2 + core, z)

    faces = [[face_of(f, d) for d in range(RING)] for f in range(2)]
    s_of = [[faces[f][d][0] for d in range(RING)] for f in (0, 1)]
    t_of = [s_of[1], s_of[0]]
    s_peer = [[faces[f][d][1] for d in range(RING)] for f in (0, 1)]
    t_peer = [s_peer[1], s_peer[0]]
    z_of = [lax.rem(z + d, n_z) for d in range(n_z)]
    z_peer = [(past, z_of[d]) for d in range(n_z)]

    loads = []

    def load(src, dst):
        copy = pltpu.make_async_copy(src, dst, load_sem.at[len(loads)])
        copy.start()
        loads.append(copy)
        return copy

    def sig_rows(b, part):
        return pl.ds(pl.multiple_of(b * rows + part * half, half), half)

    ld = {}
    ld["p0"] = load(sig_hbm.at[sig_rows(0, 1 - core)], sig.at[sig_rows(0, 1 - core)])
    first = [load(g_hbm.at[:, i * tile : (i + 1) * tile], g.at[0, :, i * tile : (i + 1) * tile]) for i in range(width // tile)]

    def load_more():
        ld["o0"] = load(sig_hbm.at[sig_rows(0, core)], sig.at[sig_rows(0, core)])
        ld["g1"] = load(g_hbm.at[:, width : 2 * width], g.at[1])

    def load_rest():
        ld["p1"] = load(sig_hbm.at[sig_rows(1, 1 - core)], sig.at[sig_rows(1, 1 - core)])
        ld["o1"] = load(sig_hbm.at[sig_rows(1, core)], sig.at[sig_rows(1, core)])
        ld["edge"] = load(edge_hbm, edge)
        ld["vol"] = load(vol_hbm, vol)
        ld["coup"] = load(coup_hbm, coup)

    barrier = pltpu.get_barrier_semaphore()
    friends = [partner] + s_peer[0][1:] + s_peer[1][1:] + z_peer[1:]
    for friend in friends:
        pl.semaphore_signal(barrier, inc=1, device_id=friend, device_id_type=MESH)

    sends = []
    ids = {}

    def sem_id(name):
        return ids.setdefault(name, len(ids))

    def put(name, src, dst, to):
        i = sem_id(name)
        copy = pltpu.make_async_remote_copy(
            src_ref=src, dst_ref=dst, send_sem=send_sem.at[i], recv_sem=recv_sem.at[i],
            device_id=to, device_id_type=MESH,
        )
        copy.start()
        sends.append(copy)

    def arrived(name, dst):
        i = sem_id(name)
        pltpu.make_async_remote_copy(
            src_ref=dst, dst_ref=dst, send_sem=send_sem.at[i], recv_sem=recv_sem.at[i],
            device_id=partner, device_id_type=MESH,
        ).wait_recv()

    def at(start, size):
        return pl.ds(pl.multiple_of(start, size), size)

    def product_send(k):
        b, j = k // 2, k % 2
        if j == 0:
            ld[f"p{b}"].wait()
        if k == 0:
            load_more()
        if k == 1:
            ld["g1"].wait()
        for i in range(width // tile):
            if k == 0:
                first[i].wait()
            cols = pl.ds(i * tile, tile)
            psend[k, :, cols] = dot(sig[sig_rows(b, 1 - core)], g[j, :, cols])
        if k == 0:
            load_rest()
            pl.semaphore_wait(barrier, len(friends))
        put(("chip", k), psend.at[k], precv.at[k], partner)

    def product_own(k):
        b, j = k // 2, k % 2
        if j == 0:
            ld[f"o{b}"].wait()
        for i in range(width // tile):
            cols = pl.ds(i * tile, tile)
            own[k, :, cols] = dot(sig[sig_rows(b, core)], g[j, :, cols])

    def row(h, d):
        return pl.multiple_of(h * (half // 2) + s_of[h][d] * sub, sub)

    def chip_sum(k):
        arrived(("chip", k), precv.at[k])
        a_buf[k] = (own[k] + precv[k]).astype(BF16)
        for d in (3, 1, 2):
            for h in range(2):
                put(("a", k, h, d), a_buf.at[k, pl.ds(row(h, d), sub)], ra.at[k, h, d - 1], s_peer[h][d])

    def ring_sum(k):
        for h in range(2):
            mine = pl.ds(row(h, 0), sub)
            t = t_of[h]
            total = own[k, mine] + precv[k, mine]
            for d in (2, 1, 3):
                arrived(("a", k, h, d), ra.at[k, h, d - 1])
                total = total + ra[k, h, d - 1].astype(F32)
            b_buf[k, h, t[0]] = total.astype(BF16)
            for d in (3, 1, 2):
                ref = b_buf.at[k, h, t[0]]
                put(("b", k, h, d), ref, ref, t_peer[h][d])

    def mem_at(k, part, h, d):
        return mem.at[k, pl.ds(pl.multiple_of(part * half + row(h, d), sub), sub)]

    def plane_sum(k):
        for h in range(2):
            for d in (2, 1, 3):
                arrived(("b", k, h, d), b_buf.at[k, h, t_of[h][d]])
            total = b_buf[k, h, 0].astype(F32)
            for i in range(1, RING):
                total = total + b_buf[k, h, i].astype(F32)
            mem[k, pl.ds(pl.multiple_of(core * half + row(h, 0), sub), sub)] = total.astype(BF16)
            ref = mem_at(k, core, h, 0)
            for d in (3, 1, 2):
                put(("c", k, h, d), ref, ref, s_peer[h][d])
            put(("f", k, h, 0), ref, ref, partner)

    def gather(k):
        for d in (2, 1, 3):
            for h in range(2):
                ref = mem_at(k, core, h, d)
                arrived(("c", k, h, d), ref)
                put(("f", k, h, d), ref, ref, partner)

    def gathered(k):
        for d in (0, 2, 1, 3):
            for h in range(2):
                arrived(("f", k, h, d), mem_at(k, 1 - core, h, d))

    def columns_of(k, i):
        return pl.ds((k % 2) * width + i * tile, tile)

    def fold(value):
        square = value * value
        part = jnp.sum(square.reshape(rows // 8, 8, tile), axis=0)
        out = part[:, 0:128]
        for i in range(1, tile // 128):
            out = out + part[:, i * 128 : (i + 1) * 128]
        return out

    def cube_of(cols, gnew):
        cube = (gnew * gnew * gnew).reshape(rows // N, N, tile) * coup[:, cols][None]
        return cube.reshape(rows, tile)

    def finish(cols, gnew):
        cube = cube_of(cols, gnew)
        cubic[:, cols] = cube
        return fold(cube)

    def share(b, total):
        stat[b, z] = total
        for d in range(1, n_z):
            put(("z", b, d), stat.at[b, z], stat.at[b, z], z_peer[d])

    def scale_of(b):
        for d in range(1, n_z):
            arrived(("z", b, d), stat.at[b, z_of[n_z - d]])
        total = jnp.sum(jnp.sum(stat[b], axis=0))
        mean = total / count_all
        return jnp.sqrt(jnp.full((8, 128), mean + 1e-6, F32))[0:1, 0:1]

    def start_value(i):
        if i == 0:
            ld["edge"].wait()
            ld["vol"].wait()
            ld["coup"].wait()
        cols = pl.ds(i * width // 2, width // 2)
        s_buf[0, :, cols] = dot(vol[0, :, rows : 2 * rows], edge[:, cols])

    def first_block(k):
        gathered(k)
        total = None
        for i in range(width // tile):
            cols = columns_of(k, i)
            gnew = s_buf[0, :, cols] + dot(vol[0, :, 0:rows], mem[k, :, pl.ds(i * tile, tile)])
            cube = cube_of(cols, gnew)
            cubic0[:, cols] = cube
            cube16[:, cols] = cube.astype(BF16)
            g_out[0:rows, cols] = gnew.astype(BF16)
            part = fold(cube)
            total = part if total is None else total + part
        return total

    def second_memory(k):
        gathered(k)
        for i in range(width // tile):
            s_buf[1, :, columns_of(k, i)] = dot(vol[1, :, 0:rows], mem[k, :, pl.ds(i * tile, tile)])

    product_send(0)
    product_own(0)
    for k in range(1, CHUNKS):
        product_send(k)
        chip_sum(k - 1)
        product_own(k)
    ring_sum(0)
    chip_sum(3)
    start_value(0)
    ring_sum(1)
    start_value(1)
    ring_sum(2)
    start_value(2)
    plane_sum(0)
    ring_sum(3)
    start_value(3)
    plane_sum(1)
    plane_sum(2)
    gather(0)
    plane_sum(3)
    gather(1)
    total = first_block(0)
    total = total + first_block(1)
    share(0, total)
    gather(2)
    gather(3)
    for i in range(2 * width // tile):
        cols = pl.ds(i * tile, tile)
        s_buf[0, :, cols] = dot(vol[1, :, rows : 2 * rows], cube16[:, cols])
    second_memory(2)
    second_memory(3)
    inv0 = 1.0 / scale_of(0)
    total = None
    for i in range(2 * width // tile):
        cols = pl.ds(i * tile, tile)
        gnew = s_buf[1, :, cols] + s_buf[0, :, cols] * inv0
        s_buf[1, :, cols] = gnew
        part = finish(cols, gnew)
        total = part if total is None else total + part
    share(1, total)
    for i in range(2 * width // tile):
        cols = pl.ds(i * tile, tile)
        g_out[rows : 2 * rows, cols] = s_buf[1, :, cols].astype(BF16)
        s_out[0:rows, cols] = (cubic0[:, cols] * inv0).astype(BF16)
    inv1 = 1.0 / scale_of(1)
    for i in range(2 * width // tile):
        cols = pl.ds(i * tile, tile)
        s_out[rows : 2 * rows, cols] = (cubic[:, cols] * inv1).astype(BF16)
    for copy in sends:
        copy.wait_send()


def write_out(g_in, s_in, g_out, s_out, sem):
    part = g_in.shape[0] // 4
    copies = []
    for i in range(4):
        for a, (src, dst) in enumerate(((g_in, g_out), (s_in, s_out))):
            here = pl.ds(i * part, part)
            copies.append(pltpu.make_async_copy(src.at[here], dst.at[here], sem.at[2 * i + a]))
            copies[-1].start()
    for copy in copies:
        copy.wait()


def per_device(g_hist, sigma_hist, volterra, sigma_edge, coupling):
    rows = volterra.shape[1]
    columns = g_hist.shape[1]
    depth = g_hist.shape[0]
    n_z = lax.axis_size("second")
    width = columns // 2
    half = rows // 2
    sub = half // 2 // RING
    n_sem = 27 * CHUNKS + 2 * (n_z - 1)
    vmem = pltpu.VMEM
    outs = pl.pallas_call(
        functools.partial(kernel, n_z, rows * columns * n_z),
        out_shape=[pltpu.VMEM((2 * rows, columns), BF16)] * 2,
        in_specs=[pl.BlockSpec(memory_space=pltpu.HBM)] * 5,
        out_specs=[pl.BlockSpec(memory_space=pltpu.VMEM)] * 2,
        scratch_shapes=[
            vmem((2, depth, width), BF16),
            vmem((2 * rows, depth), BF16),
            vmem(volterra.shape, BF16),
            vmem(sigma_edge.shape, BF16),
            vmem(coupling.shape, F32),
            vmem((CHUNKS, half, width), F32),
            vmem((CHUNKS, half, width), F32),
            vmem((CHUNKS, half, width), F32),
            vmem((CHUNKS, half, width), BF16),
            vmem((CHUNKS, 2, RING - 1, sub, width), BF16),
            vmem((CHUNKS, 2, RING, sub, width), BF16),
            vmem((CHUNKS, rows, width), BF16),
            vmem((2, rows, columns), F32),
            vmem((rows, columns), F32),
            vmem((rows, columns), F32),
            vmem((rows, columns), BF16),
            vmem((2, n_z, 8, 128), F32),
            pltpu.SemaphoreType.DMA((n_sem,)),
            pltpu.SemaphoreType.DMA((n_sem,)),
            pltpu.SemaphoreType.DMA((10,)),
        ],
        compiler_params=pltpu.CompilerParams(
            collective_id=0, has_side_effects=True, vmem_limit_bytes=62_800_000
        ),
    )(g_hist, sigma_hist, volterra, sigma_edge, coupling)
    return pl.pallas_call(
        write_out,
        out_shape=[jax.ShapeDtypeStruct((2 * rows, columns), BF16)] * 2,
        in_specs=[pl.BlockSpec(memory_space=pl.ANY)] * 2,
        out_specs=[pl.BlockSpec(memory_space=pl.ANY)] * 2,
        scratch_shapes=[pltpu.SemaphoreType.DMA((8,))],
        compiler_params=pltpu.CompilerParams(vmem_limit_bytes=1024 * 1024),
    )(*outs)


def solution(mesh):
    return jax.shard_map(
        per_device,
        mesh=mesh,
        in_specs=(P("past", "second"), P(None, "past"), P(), P(None, "second"), P(None, "second")),
        out_specs=(P(None, "second"), P(None, "second")),
        check_vma=False,
    )
```

```python
import functools

import jax
import jax.numpy as jnp
from jax import lax
from jax.experimental import pallas as pl
from jax.experimental.pallas import tpu as pltpu
from jax.sharding import PartitionSpec as P

N = 32
MESH = pl.DeviceIdType.MESH
F32 = jnp.float32
BF16 = jnp.bfloat16
RING = 4
CHUNKS = 4
ORDER = ((0, 2), (1, 2), (0, 3), (1, 3), (0, 1), (1, 1))


def dot(a, b):
    return jnp.dot(a, b, preferred_element_type=F32)


def kernel(
    n_z, count_all,
    g_hbm, sig_hbm, vol_hbm, edge_hbm, coup_hbm, g_out, s_out,
    g, sig, vol, edge, coup, psend, precv, own, a_buf, ra, b_buf, mem, s_buf, cubic0, cubic, cube16, stat,
    send_sem, recv_sem, load_sem,
):
    rows = mem.shape[1]
    half = rows // 2
    sub = half // 2 // RING
    width = mem.shape[2]
    tile = min(256, width)

    past = lax.axis_index("past")
    z = lax.axis_index("second")
    core = lax.rem(past, 2)
    x = lax.rem(past // 2, RING)
    y = past // (2 * RING)
    partner = (past + 1 - 2 * core, z)
    x_of = [lax.rem(x + d, RING) for d in range(RING)]
    y_of = [lax.rem(y + d, RING) for d in range(RING)]
    x_peer = [((y * RING + x_of[d]) * 2 + core, z) for d in range(RING)]
    y_peer = [((y_of[d] * RING + x) * 2 + core, z) for d in range(RING)]
    s_of, t_of = [x_of, y_of], [y_of, x_of]
    s_peer, t_peer = [x_peer, y_peer], [y_peer, x_peer]
    z_of = [lax.rem(z + d, n_z) for d in range(n_z)]
    z_peer = [(past, z_of[d]) for d in range(n_z)]

    loads = []

    def load(src, dst):
        copy = pltpu.make_async_copy(src, dst, load_sem.at[len(loads)])
        copy.start()
        loads.append(copy)
        return copy

    def sig_rows(b, part):
        return pl.ds(pl.multiple_of(b * rows + part * half, half), half)

    ld = {}
    ld["p0"] = load(sig_hbm.at[sig_rows(0, 1 - core)], sig.at[sig_rows(0, 1 - core)])
    first = [load(g_hbm.at[:, i * tile : (i + 1) * tile], g.at[0, :, i * tile : (i + 1) * tile]) for i in range(width // tile)]

    ld["g1"] = load(g_hbm.at[:, width : 2 * width], g.at[1])
    ld["o0"] = load(sig_hbm.at[sig_rows(0, core)], sig.at[sig_rows(0, core)])
    ld["p1"] = load(sig_hbm.at[sig_rows(1, 1 - core)], sig.at[sig_rows(1, 1 - core)])
    ld["o1"] = load(sig_hbm.at[sig_rows(1, core)], sig.at[sig_rows(1, core)])

    def load_rest():
        ld["edge"] = load(edge_hbm, edge)
        ld["vol"] = load(vol_hbm, vol)
        ld["coup"] = load(coup_hbm, coup)

    barrier = pltpu.get_barrier_semaphore()
    friends = [partner] + s_peer[0][1:] + s_peer[1][1:] + z_peer[1:]
    for friend in friends:
        pl.semaphore_signal(barrier, inc=1, device_id=friend, device_id_type=MESH)

    sends = []
    ids = {}

    def sem_id(name):
        return ids.setdefault(name, len(ids))

    def put(name, src, dst, to):
        i = sem_id(name)
        copy = pltpu.make_async_remote_copy(
            src_ref=src, dst_ref=dst, send_sem=send_sem.at[i], recv_sem=recv_sem.at[i],
            device_id=to, device_id_type=MESH,
        )
        copy.start()
        sends.append(copy)

    def arrived(name, dst):
        i = sem_id(name)
        pltpu.make_async_remote_copy(
            src_ref=dst, dst_ref=dst, send_sem=send_sem.at[i], recv_sem=recv_sem.at[i],
            device_id=partner, device_id_type=MESH,
        ).wait_recv()

    def at(start, size):
        return pl.ds(pl.multiple_of(start, size), size)

    def product_send(k):
        b, j = k // 2, k % 2
        if j == 0:
            ld[f"p{b}"].wait()
        if k == 1:
            ld["g1"].wait()
        for i in range(width // tile):
            if k == 0:
                first[i].wait()
            cols = pl.ds(i * tile, tile)
            psend[k, :, cols] = dot(sig[sig_rows(b, 1 - core)], g[j, :, cols])
        if k == 2:
            load_rest()
        if k == 0:
            pl.semaphore_wait(barrier, len(friends))
        put(("chip", k), psend.at[k], precv.at[k], partner)

    def product_own(k):
        b, j = k // 2, k % 2
        if j == 0:
            ld[f"o{b}"].wait()
        for i in range(width // tile):
            cols = pl.ds(i * tile, tile)
            own[k, :, cols] = dot(sig[sig_rows(b, core)], g[j, :, cols])

    def row(h, d):
        return pl.multiple_of(h * (half // 2) + s_of[h][d] * sub, sub)

    def chip_sum(k):
        arrived(("chip", k), precv.at[k])
        a_buf[k] = (own[k] + precv[k]).astype(BF16)
        for h, d in ORDER:
            put(("a", k, h, d), a_buf.at[k, pl.ds(row(h, d), sub)], ra.at[k, h, d - 1], s_peer[h][d])

    def ring_sum(k):
        for h in range(2):
            mine = pl.ds(row(h, 0), sub)
            t = t_of[h]
            total = own[k, mine] + precv[k, mine]
            for d in (1, 3, 2):
                arrived(("a", k, h, d), ra.at[k, h, d - 1])
                total = total + ra[k, h, d - 1].astype(F32)
            b_buf[k, h, t[0]] = total.astype(BF16)
        for h, d in ORDER:
            ref = b_buf.at[k, h, t_of[h][0]]
            put(("b", k, h, d), ref, ref, t_peer[h][d])

    def mem_at(k, part, h, d):
        return mem.at[k, pl.ds(pl.multiple_of(part * half + row(h, d), sub), sub)]

    def plane_sum(k):
        for h in range(2):
            for d in (1, 3, 2):
                arrived(("b", k, h, d), b_buf.at[k, h, t_of[h][RING - d]])
            total = b_buf[k, h, 0].astype(F32)
            for i in range(1, RING):
                total = total + b_buf[k, h, i].astype(F32)
            mem[k, pl.ds(pl.multiple_of(core * half + row(h, 0), sub), sub)] = total.astype(BF16)
        for h, d in ORDER:
            ref = mem_at(k, core, h, 0)
            put(("c", k, h, d), ref, ref, s_peer[h][d])

    def gather(k):
        for h in range(2):
            ref = mem_at(k, core, h, 0)
            put(("f", k, h, 0), ref, ref, partner)
        for d in (1, 3, 2):
            for h in range(2):
                ref = mem_at(k, core, h, RING - d)
                arrived(("c", k, h, d), ref)
                put(("f", k, h, RING - d), ref, ref, partner)

    def gathered(k):
        for d in (0, 3, 1, 2):
            for h in range(2):
                arrived(("f", k, h, d), mem_at(k, 1 - core, h, d))

    def columns_of(k, i):
        return pl.ds((k % 2) * width + i * tile, tile)

    def fold(value):
        square = value * value
        part = jnp.sum(square.reshape(rows // 8, 8, tile), axis=0)
        out = part[:, 0:128]
        for i in range(1, tile // 128):
            out = out + part[:, i * 128 : (i + 1) * 128]
        return out

    def cube_of(cols, gnew):
        cube = (gnew * gnew * gnew).reshape(rows // N, N, tile) * coup[:, cols][None]
        return cube.reshape(rows, tile)

    def share(b, total):
        stat[b, z] = total
        for d in range(1, n_z):
            put(("z", b, d), stat.at[b, z], stat.at[b, z], z_peer[d])

    def scale_of(b):
        for d in range(1, n_z):
            arrived(("z", b, d), stat.at[b, z_of[n_z - d]])
        total = jnp.sum(jnp.sum(stat[b], axis=0))
        mean = total / count_all
        return jnp.sqrt(jnp.full((8, 128), mean + 1e-6, F32))[0:1, 0:1]

    def start_value(i):
        if i == 0:
            ld["edge"].wait()
            ld["vol"].wait()
            ld["coup"].wait()
        cols = pl.ds(i * width // 2, width // 2)
        s_buf[0, :, cols] = dot(vol[0, :, rows : 2 * rows], edge[:, cols])

    def first_block(k):
        gathered(k)
        total = None
        for i in range(width // tile):
            cols = columns_of(k, i)
            gnew = s_buf[0, :, cols] + dot(vol[0, :, 0:rows], mem[k, :, pl.ds(i * tile, tile)])
            cubic0[:, cols] = gnew
            part = fold(cube_of(cols, gnew))
            total = part if total is None else total + part
        return total

    def second_memory(k):
        gathered(k)
        for i in range(width // tile):
            s_buf[1, :, columns_of(k, i)] = dot(vol[1, :, 0:rows], mem[k, :, pl.ds(i * tile, tile)])

    for b in range(2):
        product_send(2 * b)
        product_send(2 * b + 1)
        for k in (2 * b, 2 * b + 1):
            product_own(k)
            chip_sum(k)
    for i in range(4):
        start_value(i)
    ring_sum(0)
    ring_sum(1)
    ring_sum(2)
    plane_sum(0)
    ring_sum(3)
    plane_sum(1)
    plane_sum(2)
    gather(0)
    plane_sum(3)
    gather(1)
    total = first_block(0)
    total = total + first_block(1)
    share(0, total)
    gather(2)
    gather(3)
    for i in range(2 * width // tile):
        cols = pl.ds(i * tile, tile)
        gnew = cubic0[:, cols]
        g_out[0:rows, cols] = gnew.astype(BF16)
        cube = cube_of(cols, gnew)
        cubic0[:, cols] = cube
        cube16[:, cols] = cube.astype(BF16)
    for i in range(2 * width // tile):
        cols = pl.ds(i * tile, tile)
        s_buf[0, :, cols] = dot(vol[1, :, rows : 2 * rows], cube16[:, cols])
    second_memory(2)
    second_memory(3)
    inv0 = 1.0 / scale_of(0)
    total = None
    for i in range(2 * width // tile):
        cols = pl.ds(i * tile, tile)
        gnew = s_buf[1, :, cols] + s_buf[0, :, cols] * inv0
        s_buf[1, :, cols] = gnew
        part = fold(cube_of(cols, gnew))
        total = part if total is None else total + part
    share(1, total)
    for i in range(2 * width // tile):
        cols = pl.ds(i * tile, tile)
        gnew = s_buf[1, :, cols]
        g_out[rows : 2 * rows, cols] = gnew.astype(BF16)
        cubic[:, cols] = cube_of(cols, gnew)
        s_out[0:rows, cols] = (cubic0[:, cols] * inv0).astype(BF16)
    inv1 = 1.0 / scale_of(1)
    for i in range(2 * width // tile):
        cols = pl.ds(i * tile, tile)
        s_out[rows : 2 * rows, cols] = (cubic[:, cols] * inv1).astype(BF16)
    for copy in sends:
        copy.wait_send()


def write_out(g_in, s_in, g_out, s_out, sem):
    part = g_in.shape[0] // 4
    copies = []
    for i in range(4):
        for a, (src, dst) in enumerate(((g_in, g_out), (s_in, s_out))):
            here = pl.ds(i * part, part)
            copies.append(pltpu.make_async_copy(src.at[here], dst.at[here], sem.at[2 * i + a]))
            copies[-1].start()
    for copy in copies:
        copy.wait()


def per_device(g_hist, sigma_hist, volterra, sigma_edge, coupling):
    rows = volterra.shape[1]
    columns = g_hist.shape[1]
    depth = g_hist.shape[0]
    n_z = lax.axis_size("second")
    width = columns // 2
    half = rows // 2
    sub = half // 2 // RING
    n_sem = 27 * CHUNKS + 2 * (n_z - 1)
    vmem = pltpu.VMEM
    outs = pl.pallas_call(
        functools.partial(kernel, n_z, rows * columns * n_z),
        out_shape=[pltpu.VMEM((2 * rows, columns), BF16)] * 2,
        in_specs=[pl.BlockSpec(memory_space=pltpu.HBM)] * 5,
        out_specs=[pl.BlockSpec(memory_space=pltpu.VMEM)] * 2,
        scratch_shapes=[
            vmem((2, depth, width), BF16),
            vmem((2 * rows, depth), BF16),
            vmem(volterra.shape, BF16),
            vmem(sigma_edge.shape, BF16),
            vmem(coupling.shape, F32),
            vmem((CHUNKS, half, width), F32),
            vmem((CHUNKS, half, width), F32),
            vmem((CHUNKS, half, width), F32),
            vmem((CHUNKS, half, width), BF16),
            vmem((CHUNKS, 2, RING - 1, sub, width), BF16),
            vmem((CHUNKS, 2, RING, sub, width), BF16),
            vmem((CHUNKS, rows, width), BF16),
            vmem((2, rows, columns), F32),
            vmem((rows, columns), F32),
            vmem((rows, columns), F32),
            vmem((rows, columns), BF16),
            vmem((2, n_z, 8, 128), F32),
            pltpu.SemaphoreType.DMA((n_sem,)),
            pltpu.SemaphoreType.DMA((n_sem,)),
            pltpu.SemaphoreType.DMA((10,)),
        ],
        compiler_params=pltpu.CompilerParams(
            collective_id=0, has_side_effects=True, vmem_limit_bytes=62_800_000
        ),
    )(g_hist, sigma_hist, volterra, sigma_edge, coupling)
    return pl.pallas_call(
        write_out,
        out_shape=[jax.ShapeDtypeStruct((2 * rows, columns), BF16)] * 2,
        in_specs=[pl.BlockSpec(memory_space=pl.ANY)] * 2,
        out_specs=[pl.BlockSpec(memory_space=pl.ANY)] * 2,
        scratch_shapes=[pltpu.SemaphoreType.DMA((8,))],
        compiler_params=pltpu.CompilerParams(vmem_limit_bytes=1024 * 1024),
    )(*outs)


def solution(mesh):
    return jax.shard_map(
        per_device,
        mesh=mesh,
        in_specs=(P("past", "second"), P(None, "past"), P(), P(None, "second"), P(None, "second")),
        out_specs=(P(None, "second"), P(None, "second")),
        check_vma=False,
    )
```
